32 devices in a mesh: grp: 2 (over x), freq: 16 (over z, y, core).
Axes of the slice: x: 2, y: 2, z: 4, core: 2. Of those that a mesh axis runs over, the one named last changes fastest.
Arguments:
- start_field: bfloat16 [512, 384, 512], P(('grp', 'freq')), parts along dimension 0, may hold values from -2.390625 to 2.390625
- recorded: bfloat16 [32, 384, 4, 128], P(('grp', 'freq')), parts along dimension 0, may hold values from -6 to 6
- multiples: bfloat16 [32, 4, 3, 64, 128], P(('grp', 'freq')), parts along dimension 0, may hold values from -0.3125 to 0.3125
- block_index: int32 [4, 3], replicated, may hold values from 0 to 3, all different within a row
- radius: int32 [512, 384], P(('grp', 'freq')), parts along dimension 0, may hold values from 0 to 4
Outputs:
- field: float32 [512, 384, 512], P(('grp', 'freq')), parts along dimension 0
- residual: float32 [32, 384, 4, 128], P(('grp', 'freq')), parts along dimension 0
The draws below stay inside these ranges and needn't reach their ends.
There are 2 independent parts, one for each index of `grp`. The reference program is written for one: setup_inputs(seed, part) draws one part's arguments, and reference() takes and returns one part's arrays. A program takes and returns all parts, laid end to end along the dimension named above; an argument that names none is the same for every part. Nothing has to cross between parts.
Inputs may be any that keep to these rules, and one draw needn't show every extreme that they name: `block_index`: each row names 3 different source blocks, and every block is named by some row.
All inputs are finite; a program needn't handle non-finite values.
Results may differ from the reference program's by a relative error of at most 0.004.
Values may be sent and summed in bfloat16 or wider, within the bound.
A program may use at most 64 MiB of HBM per device.

```python
import math
import jax
import jax.numpy as jnp
from jax import lax

NB = 4
BS = 64
BANDS = 3
NT = 512
RADIUS = 4
ITERS = 2
RECV = 384
S = 256
FREQ = 16


def draw_radius(key, part):
    uniform_pick = jax.random.randint(key, (S, RECV), 0, RADIUS + 1)
    source_ids = jnp.arange(S, dtype=jnp.int32)[:, None]
    receiver_ids = jnp.arange(RECV, dtype=jnp.int32)[None, :]
    return jnp.where((source_ids * 7 + receiver_ids) % 11 == 0, RADIUS, uniform_pick).astype(jnp.int32)


def shard_levels(key, shape, shards, least, top_value):
    factor_of, own = 1.0, jax.random.fold_in(key, 6)
    for dim, blocks in shards:
        steps = jnp.exp(jax.random.uniform(jax.random.fold_in(own, dim), (blocks,), jnp.float32, least / len(shards), top_value / len(shards)))
        factor_of = factor_of * jnp.repeat(steps, shape[dim] // blocks).reshape([-1 if axis == dim else 1 for axis in range(len(shape))])
    return factor_of


def picks_of(own_key, rows, amount, top, lift):
    order = jax.random.permutation(jax.random.fold_in(own_key, 1), amount)
    boost = order
    for power in range(3):
        boost = boost * boost // amount
    boost = boost * lift // amount
    tickets = jax.random.randint(jax.random.fold_in(own_key, 2), (rows, amount), 0, 4096) + boost
    fixed_rows = jax.random.permutation(jax.random.fold_in(own_key, 3), rows)[jnp.arange(amount) % rows]
    tickets = jnp.where(jnp.arange(rows)[:, None] == fixed_rows[None, :], 1 << 14, tickets)
    merit = tickets * amount + jnp.arange(amount)
    return lax.top_k(merit.astype(jnp.int32), top)[1].astype(jnp.int32)


def bell_draw(key, extent, spread, most, cuts=(), kind=jnp.bfloat16):
    array = jax.random.normal(key, extent, jnp.float32) * spread
    if len(cuts) > 0:
        array = shard_levels(key, extent, cuts, -0.22, 0.18) * array
    return jnp.clip(array, min=-most, max=most).astype(kind)


def setup_inputs(seed: int = 0, part: int = 0) -> dict:
    arg_keys = jax.random.split(jax.random.key(seed), 6)
    own_keys = jax.random.split(jax.random.fold_in(arg_keys[5], part), 6)
    start_field = bell_draw(own_keys[0], (S, RECV, NT), 0.3, 2.390625, ((0, 16),))
    recorded = bell_draw(own_keys[1], (FREQ, RECV, NB, 2 * BS), 1.0, 6.0, ((0, 16),))
    multiples = bell_draw(own_keys[2], (FREQ, NB, BANDS, BS, 2 * BS), (2 * BANDS * BS) ** -0.5, 0.3125, ((0, 16),))
    block_index = picks_of(arg_keys[3], NB, NB, BANDS, 0)
    radius = draw_radius(jax.random.fold_in(jax.random.fold_in(arg_keys[5], part), 71), part)
    return dict(start_field=start_field, recorded=recorded, multiples=multiples, block_index=block_index, radius=radius)


step_size = 0.5
shrinkage = 0.05

def dft_table(freq_count):
    sample_ids = jnp.arange(NT, dtype=jnp.int32)
    bin_ids = jnp.arange(freq_count, dtype=jnp.int32) + 1
    phases = sample_ids[:, None] * bin_ids[None, :] % NT
    angles = phases.astype(jnp.float32) * (2.0 * math.pi / NT)
    stacked = jnp.stack([jnp.cos(angles), -jnp.sin(angles)], axis=-1)
    return stacked.reshape(NT, 2 * freq_count) / math.sqrt(NT)

def embed_complex(multiples):
    real_part = multiples[..., :BS]
    imag_part = multiples[..., BS:]
    upper_rows = jnp.concatenate([real_part, imag_part], axis=-1)
    lower_rows = jnp.concatenate([-imag_part, real_part], axis=-1)
    return jnp.concatenate([upper_rows, lower_rows], axis=-2)

def owner_layout(arrived, freq_count):
    shaped = arrived.reshape(freq_count, 2, NB, BS, arrived.shape[2])
    return shaped.transpose(0, 4, 2, 1, 3).reshape(freq_count, arrived.shape[2], NB, 2 * BS)

def trace_layout(backward, freq_count):
    shaped = backward.reshape(freq_count, backward.shape[1], NB, 2, BS)
    return shaped.transpose(0, 3, 2, 4, 1).reshape(2 * freq_count, NB * BS, backward.shape[1])

def smooth_along(extended, radius, rows_out, along):
    shares = 1.0 / (2.0 * radius.astype(jnp.float32) + 1.0)
    summed = None
    for offset in range(-RADIUS, RADIUS + 1):
        weight = jnp.where(abs(offset) <= radius, shares, 0.0)
        if along == 0:
            weight = weight[:, :, None]
        else:
            weight = weight[None, :, :]
        piece = lax.slice_in_dim(extended, RADIUS + offset, RADIUS + offset + rows_out, axis=along)
        term = weight * piece.astype(jnp.float32)
        summed = term if summed is None else summed + term
    return summed

def reference(start_field, recorded, multiples, block_index, radius):
    basis = dft_table(FREQ)
    operator = embed_complex(multiples).astype(jnp.float32)
    field = start_field.astype(jnp.float32)
    residual = None
    for sweep in range(ITERS):
        spectra = jnp.einsum('srt,tc->csr', field, basis, precision=lax.Precision.HIGHEST).astype(jnp.bfloat16)
        spectra = lax.optimization_barrier(spectra)
        owned = owner_layout(spectra, FREQ).astype(jnp.float32)
        predicted = []
        for out_block in range(NB):
            summed = jnp.zeros((FREQ, RECV, 2 * BS), jnp.float32)
            for band_id in range(BANDS):
                source = owned[:, :, block_index[out_block, band_id]]
                summed = summed + jnp.einsum('frc,fcd->frd', source, operator[:, out_block, band_id])
            predicted.append(summed)
        residual = recorded.astype(jnp.float32) - jnp.stack(predicted, axis=2)
        narrow = lax.optimization_barrier(residual.astype(jnp.bfloat16)).astype(jnp.float32)
        backward = jnp.zeros((FREQ, RECV, NB, 2 * BS), jnp.float32)
        for out_block in range(NB):
            for band_id in range(BANDS):
                contrib = jnp.einsum('frd,fcd->frc', narrow[:, :, out_block], operator[:, out_block, band_id])
                backward = backward.at[:, :, block_index[out_block, band_id]].add(contrib)
        returned = lax.optimization_barrier(trace_layout(backward.astype(jnp.bfloat16), FREQ)).astype(jnp.float32)
        gradient = jnp.einsum('csr,tc->srt', returned, basis, precision=lax.Precision.HIGHEST)
        extended = jnp.pad(gradient, ((RADIUS, RADIUS), (0, 0), (0, 0)))
        smoothed = smooth_along(extended, radius, S, 0)
        update = field + step_size * smoothed
        field = jnp.sign(update) * jnp.maximum(jnp.abs(update) - shrinkage, 0.0)
    return (field, residual)
```

```python
import functools
import math

import jax
import jax.numpy as jnp
import numpy as np
from jax import lax
from jax.experimental import pallas as pl
from jax.experimental.pallas import tpu as pltpu
from jax.sharding import PartitionSpec as P

NB = 4
BS = 64
BANDS = 3
RADIUS = 4

step_size = 0.5
shrinkage = 0.05

BF16 = jnp.bfloat16
F32 = jnp.float32


def dft_table(freq_count, samples):
    phases = (np.arange(samples)[:, None] * (np.arange(freq_count) + 1)[None, :]) % samples
    angles = phases.astype(np.float64) * (2.0 * math.pi / samples)
    stacked = np.stack([np.cos(angles), -np.sin(angles)], axis=-1)
    return (stacked.reshape(samples, 2 * freq_count) / math.sqrt(samples)).astype(np.float32)


def halves(table):
    high = jnp.asarray(table).astype(BF16)
    low = (jnp.asarray(table) - high.astype(F32)).astype(BF16)
    return high, low


def embed_complex(multiples):
    real_part = multiples[..., :BS]
    imag_part = multiples[..., BS:]
    upper_rows = jnp.concatenate([real_part, imag_part], axis=-1)
    lower_rows = jnp.concatenate([-imag_part, real_part], axis=-1)
    return jnp.stack([upper_rows, lower_rows], axis=-3)


def dense_operators(multiples, block_index, devices, local_src):
    local_freq = multiples.shape[0]
    op = embed_complex(multiples)
    dense = None
    blocks = jnp.arange(NB, dtype=block_index.dtype)
    for band in range(BANDS):
        hit = block_index[:, band][None, :] == blocks[:, None]
        term = jnp.where(hit[None, :, None, None, :, None], op[:, :, band].transpose(0, 2, 3, 1, 4)[:, None], 0)
        dense = term if dense is None else dense + term
    sources = NB * BS
    by_part = dense.transpose(0, 2, 1, 3, 4, 5).reshape(local_freq, 2, sources, NB * 2 * BS)
    padded = jnp.pad(by_part, ((0, 0), (0, 0), (RADIUS, RADIUS), (0, 0)))
    inner = by_part.reshape(local_freq, 2, devices, local_src, NB * 2 * BS).transpose(0, 2, 1, 3, 4)
    reach = local_src + 2 * RADIUS
    outer = jnp.stack([padded[:, :, d * local_src : d * local_src + reach] for d in range(devices)], axis=1)
    columns = NB * 2 * BS
    return (
        inner.reshape(local_freq, devices * 2 * local_src, columns),
        outer.reshape(local_freq, devices * 2 * reach, columns),
    )


def soft(update):
    return update - jnp.clip(update, -shrinkage, shrinkage)


def nt_dot(a, b):
    return lax.dot_general(a, b, (((1,), (1,)), ((), ())), preferred_element_type=F32)


def tn_dot(a, b):
    return lax.dot_general(a, b, (((0,), (0,)), ((), ())), preferred_element_type=F32)


def sweeps_kernel(
    devices, chunks, width,
    start_hbm, recorded_ref, inner_ref, outer_ref, radius_ref, analysis_ref, synthesis_ref,
    first_ref, second_ref, residual_ref,
    field, wide, reach_wide, out_slabs, in_slabs, back_slabs, edge_slabs,
    load_sem, send_sem, recv_sem,
):
    me = lax.axis_index("freq")
    local_src = start_hbm.shape[0]
    local_freq = recorded_ref.shape[0]
    rows = analysis_ref.shape[0] // 2
    reach = local_src + 2 * RADIUS

    def load(c):
        return pltpu.make_async_copy(start_hbm.at[:, pl.ds(c * width, width), :], field.at[c], load_sem.at[c])

    for c in range(chunks):
        load(c).start()
    barrier = pltpu.get_barrier_semaphore()
    for shift in range(1, devices):
        pl.semaphore_signal(
            barrier, inc=1, device_id={"freq": lax.rem(me + shift, devices)}, device_id_type=pl.DeviceIdType.MESH
        )

    def exchange(phase, c, sources, targets):
        slot = phase * chunks + c

        def send(step, carry):
            peer = lax.rem(me + step, devices)
            pltpu.make_async_remote_copy(
                src_ref=sources.at[(phase // 2) * chunks + c, peer],
                dst_ref=targets.at[(phase // 2) * chunks + c, me],
                send_sem=send_sem.at[slot],
                recv_sem=recv_sem.at[slot],
                device_id={"freq": peer},
                device_id_type=pl.DeviceIdType.MESH,
            ).start()
            return carry

        lax.fori_loop(1, devices, send, 0)
        targets[(phase // 2) * chunks + c, me] = sources[(phase // 2) * chunks + c, me]

    def await_all(phase, c, refs, sems):
        whole = refs.at[(phase // 2) * chunks + c, pl.ds(0, devices - 1)]
        pltpu.make_async_copy(whole, whole, sems.at[phase * chunks + c]).wait()

    def analyse(s, samples):
        both = nt_dot(analysis_ref[...], samples)
        wide[pl.ds(s, rows, stride=local_src), :] = both[:rows] + both[rows:]

    def ship(sweep, c):
        slabs = wide[...].reshape(devices, local_freq * 2 * local_src, width)
        out_slabs[sweep * chunks + c] = slabs.astype(BF16)
        if sweep == 0 and c == 0:
            pl.semaphore_wait(barrier, devices - 1)
        exchange(2 * sweep, c, out_slabs, in_slabs)

    def own(sweep, c):
        await_all(2 * sweep, c, in_slabs, recv_sem)
        arrived = in_slabs[sweep * chunks + c].astype(F32)
        backs = []
        for f in range(local_freq):
            part = arrived[:, f * 2 * local_src : (f + 1) * 2 * local_src]
            owned = part.reshape(devices * 2 * local_src, width).T.astype(BF16)
            predicted = jnp.dot(owned, inner_ref[f], preferred_element_type=F32)
            residual = recorded_ref[f, pl.ds(c * width, width), :].astype(F32) - predicted
            if sweep == 1:
                residual_ref[f, pl.ds(c * width, width), :] = residual
            back = nt_dot(outer_ref[f], residual.astype(BF16))
            backs.append(back.reshape(devices, 2 * reach, width))
        back = backs[0] if local_freq == 1 else jnp.concatenate(backs, axis=1)
        back_slabs[sweep * chunks + c] = back.astype(BF16)
        exchange(2 * sweep + 1, c, back_slabs, edge_slabs)

    def trace_side(sweep, c, stack_ref):
        await_all(2 * sweep + 1, c, edge_slabs, recv_sem)
        reach_wide[...] = edge_slabs[sweep * chunks + c].astype(F32).reshape(rows * reach, width)

        def source(s, carry):
            span = radius_ref[s, :, pl.ds(c * width, width)]
            tap = lambda offset: reach_wide[pl.ds(s + RADIUS + offset, rows, stride=reach), :]
            box = tap(0)
            smoothed = box
            for offset in range(1, RADIUS + 1):
                box = box + (tap(offset) + tap(-offset))
                smoothed = jnp.where(span >= offset, box, smoothed)
            smoothed = smoothed * (1.0 / (2.0 * span.astype(F32) + 1.0))
            high = smoothed.astype(BF16)
            low = (smoothed - high.astype(F32)).astype(BF16)
            stack = jnp.concatenate([high, low, high], axis=0)
            stack_ref[s, :, pl.ds(c * width, width)] = stack
            if sweep == 0:
                update = field[c, s].astype(F32) + tn_dot(stack, synthesis_ref[...])
                analyse(s, soft(update).astype(BF16))
            return carry

        lax.fori_loop(0, local_src, source, 0, unroll=2)
        if sweep == 0:
            ship(1, c)

    for c in range(chunks):
        load(c).wait()

        def source(s, carry):
            analyse(s, field[c, s])
            return carry

        lax.fori_loop(0, local_src, source, 0, unroll=4)
        ship(0, c)
    for c in range(chunks):
        own(0, c)
    for c in range(chunks):
        trace_side(0, c, first_ref)
    for c in range(chunks):
        own(1, c)
    for c in range(chunks):
        trace_side(1, c, second_ref)
    for phase in range(4):
        for c in range(chunks):
            await_all(phase, c, back_slabs if phase % 2 else out_slabs, send_sem)


def finish_kernel(start_ref, first_ref, second_ref, synthesis_ref, field_ref):
    table = synthesis_ref[...]
    once = soft(start_ref[0].astype(F32) + tn_dot(first_ref[0], table))
    field_ref[0] = soft(once + tn_dot(second_ref[0], table))


def on_device(devices, start_field, recorded, multiples, block_index, radius):
    local_src, receivers, samples = start_field.shape
    local_freq = recorded.shape[0]
    columns = NB * 2 * BS
    rows = 2 * local_freq * devices
    width = 128
    chunks = receivers // width
    reach = local_src + 2 * RADIUS
    table = dft_table(local_freq * devices, samples)
    analysis = jnp.concatenate(halves(table.T), axis=0)
    high, low = halves(step_size * table.T)
    synthesis = jnp.concatenate([high, high, low], axis=0)
    inner, outer = dense_operators(multiples, block_index, devices, local_src)
    vmem = pl.BlockSpec(memory_space=pltpu.VMEM)
    slab = lambda height: pltpu.VMEM((2 * chunks, devices, local_freq * 2 * height, width), BF16)
    stack_shape = jax.ShapeDtypeStruct((local_src, 3 * rows, receivers), BF16)
    first, second, residual = pl.pallas_call(
        functools.partial(sweeps_kernel, devices, chunks, width),
        out_shape=(stack_shape, stack_shape, jax.ShapeDtypeStruct((local_freq, receivers, columns), F32)),
        in_specs=[pl.BlockSpec(memory_space=pl.ANY)] + [vmem] * 6,
        out_specs=(vmem, vmem, vmem),
        scratch_shapes=[
            pltpu.VMEM((chunks, local_src, width, samples), BF16),
            pltpu.VMEM((rows * local_src, width), F32),
            pltpu.VMEM((rows * reach, width), F32),
            slab(local_src),
            slab(local_src),
            slab(reach),
            slab(reach),
            pltpu.SemaphoreType.DMA((chunks,)),
            pltpu.SemaphoreType.DMA((4 * chunks,)),
            pltpu.SemaphoreType.DMA((4 * chunks,)),
        ],
        compiler_params=pltpu.CompilerParams(
            collective_id=0, has_side_effects=True, vmem_limit_bytes=48 << 20
        ),
    )(start_field, recorded.reshape(local_freq, receivers, columns), inner, outer,
      radius.reshape(local_src, 1, receivers), analysis, synthesis)
    field = pl.pallas_call(
        finish_kernel,
        grid=(local_src,),
        out_shape=jax.ShapeDtypeStruct(start_field.shape, F32),
        in_specs=[
            pl.BlockSpec((1, receivers, samples), lambda s: (s, 0, 0)),
            pl.BlockSpec((1, 3 * rows, receivers), lambda s: (s, 0, 0)),
            pl.BlockSpec((1, 3 * rows, receivers), lambda s: (s, 0, 0)),
            pl.BlockSpec((3 * rows, samples), lambda s: (0, 0)),
        ],
        out_specs=pl.BlockSpec((1, receivers, samples), lambda s: (s, 0, 0)),
    )(start_field, first, second, synthesis)
    return field, residual.reshape(recorded.shape)


def solution(mesh):
    placed = (
        P(("grp", "freq"), None, None),
        P(("grp", "freq"), None, None, None),
        P(("grp", "freq"), None, None, None, None),
        P(),
        P(("grp", "freq"), None),
    )
    return jax.shard_map(
        functools.partial(on_device, mesh.shape["freq"]),
        mesh=mesh,
        in_specs=placed,
        out_specs=(P(("grp", "freq"), None, None), P(("grp", "freq"), None, None, None)),
        check_vma=False,
    )
```

```python
import functools
import math

import jax
import jax.numpy as jnp
import numpy as np
from jax import lax
from jax.experimental import pallas as pl
from jax.experimental.pallas import tpu as pltpu
from jax.sharding import PartitionSpec as P

NB = 4
BS = 64
BANDS = 3
RADIUS = 4

step_size = 0.5
shrinkage = 0.05

BF16 = jnp.bfloat16
F32 = jnp.float32


def dft_table(freq_count, samples):
    phases = (np.arange(samples)[:, None] * (np.arange(freq_count) + 1)[None, :]) % samples
    angles = phases.astype(np.float64) * (2.0 * math.pi / samples)
    stacked = np.stack([np.cos(angles), -np.sin(angles)], axis=-1)
    return (stacked.reshape(samples, 2 * freq_count) / math.sqrt(samples)).astype(np.float32)


def halves(table):
    high = jnp.asarray(table).astype(BF16)
    low = (jnp.asarray(table) - high.astype(F32)).astype(BF16)
    return high, low


def soft(update):
    return update - jnp.clip(update, -shrinkage, shrinkage)


def nt_dot(a, b):
    return lax.dot_general(a, b, (((1,), (1,)), ((), ())), preferred_element_type=F32)


def tn_dot(a, b):
    return lax.dot_general(a, b, (((0,), (0,)), ((), ())), preferred_element_type=F32)


def build_operator(block_ref, multiples_ref, inner, local_src):
    parts = BS // local_src
    for f in range(multiples_ref.shape[0]):
        for j in range(NB):
            terms = [multiples_ref[f, j, b].astype(F32) for b in range(BANDS)]
            for m in range(NB):
                block = None
                for b in range(BANDS):
                    term = terms[b] * jnp.where(block_ref[j, b] == m, 1.0, 0.0)
                    block = term if block is None else block + term
                turned = jnp.concatenate([-block[:, BS:], block[:, :BS]], axis=1)
                for q in range(parts):
                    for c, half in enumerate((block, turned)):
                        row = ((m * parts + q) * 2 + c) * local_src
                        piece = half[q * local_src : (q + 1) * local_src]
                        inner[f, row : row + local_src, j * 2 * BS : (j + 1) * 2 * BS] = piece.astype(BF16)


def sweeps_kernel(
    devices, chunks, width,
    block_ref, start_hbm, recorded_ref, multiples_ref, radius_ref, analysis_ref, synthesis_ref,
    field_ref, last_ref, residual_ref,
    field, wide, flat, near, spans, given, inner, out_slabs, in_slabs, back_slabs, edge_slabs, rim_out, rim_in,
    load_sem, send_sem, recv_sem, rim_send, rim_recv,
):
    me = lax.axis_index("freq")
    local_src = start_hbm.shape[0]
    local_freq = multiples_ref.shape[0]
    rows = analysis_ref.shape[0] // 2
    block_cols = 2 * BS

    def load(c):
        return pltpu.make_async_copy(start_hbm.at[:, pl.ds(c * width, width), :], field.at[c], load_sem.at[c])

    for c in range(chunks):
        load(c).start()
    barrier = pltpu.get_barrier_semaphore()
    for shift in range(1, devices):
        pl.semaphore_signal(
            barrier, inc=1, device_id={"freq": lax.rem(me + shift, devices)}, device_id_type=pl.DeviceIdType.MESH
        )

    def exchange(phase, c, sources, targets):
        slot = phase * chunks + c
        place = (phase // 2) * chunks + c

        def send(step, carry):
            peer = lax.rem(me + step, devices)
            pltpu.make_async_remote_copy(
                src_ref=sources.at[place, peer],
                dst_ref=targets.at[place, me],
                send_sem=send_sem.at[slot],
                recv_sem=recv_sem.at[slot],
                device_id={"freq": peer},
                device_id_type=pl.DeviceIdType.MESH,
            ).start()
            return carry

        lax.fori_loop(1, devices, send, 0)
        targets[place, me] = sources[place, me]

    def await_all(phase, c, refs, sems):
        whole = refs.at[(phase // 2) * chunks + c, pl.ds(0, devices - 1)]
        pltpu.make_async_copy(whole, whole, sems.at[phase * chunks + c]).wait()

    def rim(place, side):
        return pltpu.make_async_remote_copy(
            src_ref=rim_out.at[place, side],
            dst_ref=rim_in.at[place, side],
            send_sem=rim_send.at[place, side],
            recv_sem=rim_recv.at[place, side],
            device_id={"freq": lax.rem(me + (1 if side == 0 else devices - 1), devices)},
            device_id_type=pl.DeviceIdType.MESH,
        )

    sends = (me < devices - 1, me > 0)
    gets = (me > 0, me < devices - 1)

    def analyse(s, samples):
        both = nt_dot(analysis_ref[...], samples)
        wide[pl.ds(s, rows, stride=local_src), :] = both[:rows] + both[rows:]

    def ship(sweep, c):
        slabs = wide[...].reshape(devices, local_freq * 2 * local_src, width)
        out_slabs[sweep * chunks + c] = slabs.astype(BF16)
        if sweep == 0 and c == 0:
            pl.semaphore_wait(barrier, devices - 1)
        exchange(2 * sweep, c, out_slabs, in_slabs)

    def own(sweep, c):
        await_all(2 * sweep, c, in_slabs, recv_sem)
        arrived = in_slabs[sweep * chunks + c].astype(F32)
        backs = []
        for f in range(local_freq):
            part = arrived[:, f * 2 * local_src : (f + 1) * 2 * local_src]
            owned = part.reshape(devices * 2 * local_src, width).T.astype(BF16)
            predicted = jnp.dot(owned, inner[f], preferred_element_type=F32)
            given[...] = recorded_ref[f, pl.ds(c * width * NB, width * NB), :].astype(F32)
            narrow = []
            for j in range(NB):
                left = given[pl.ds(j, width, stride=NB), :] - predicted[:, j * block_cols : (j + 1) * block_cols]
                if sweep == 1:
                    residual_ref[f, pl.ds(c * width * NB + j, width, stride=NB), :] = left
                narrow.append(left.astype(BF16))
            back = nt_dot(inner[f], jnp.concatenate(narrow, axis=1))
            backs.append(back.reshape(devices, 2 * local_src, width))
        back = backs[0] if local_freq == 1 else jnp.concatenate(backs, axis=1)
        back_slabs[sweep * chunks + c] = back.astype(BF16)
        exchange(2 * sweep + 1, c, back_slabs, edge_slabs)

    def trace_side(sweep, c):
        place = sweep * chunks + c
        await_all(2 * sweep + 1, c, edge_slabs, recv_sem)
        flat[...] = edge_slabs[place].astype(F32).reshape(rows * local_src, width)
        for s in range(local_src):
            near[RADIUS + s] = flat[pl.ds(s, rows, stride=local_src), :]
        rim_out[place, 0] = near[local_src : local_src + RADIUS].astype(BF16)
        rim_out[place, 1] = near[RADIUS : 2 * RADIUS].astype(BF16)
        for side in range(2):

            @pl.when(sends[side])
            def _():
                rim(place, side).start()

        span_lanes = pl.ds(c * width, width)

        def source(s, carry):
            span = spans[s, :, span_lanes]
            box = near[s + RADIUS]
            smoothed = box
            for offset in range(1, RADIUS + 1):
                box = box + (near[s + RADIUS + offset] + near[s + RADIUS - offset])
                smoothed = jnp.where(span >= offset, box, smoothed)
            smoothed = smoothed * (1.0 / (2.0 * span.astype(F32) + 1.0))
            high = smoothed.astype(BF16)
            low = (smoothed - high.astype(F32)).astype(BF16)
            stack = jnp.concatenate([high, low, high], axis=0)
            if sweep == 0:
                update = soft(field[c, s].astype(F32) + tn_dot(stack, synthesis_ref[...]))
                field_ref[s, span_lanes, :] = update
                analyse(s, update.astype(BF16))
            elif c < chunks - 1:
                field_ref[s, span_lanes, :] = soft(field_ref[s, span_lanes, :] + tn_dot(stack, synthesis_ref[...]))
            else:
                last_ref[s] = stack
            return carry

        low_end = min(RADIUS, local_src)
        high_end = max(local_src - RADIUS, low_end)
        lax.fori_loop(low_end, high_end, source, 0, unroll=2)
        for side in range(2):

            @pl.when(gets[side])
            def _():
                rim(place, side).wait_recv()
                at = 0 if side == 0 else RADIUS + local_src
                near[at : at + RADIUS] = rim_in[place, side].astype(F32)

        lax.fori_loop(0, low_end, source, 0, unroll=2)
        lax.fori_loop(high_end, local_src, source, 0, unroll=2)
        if sweep == 0:
            ship(1, c)

    for c in range(chunks):
        load(c).wait()

        def source(s, carry):
            analyse(s, field[c, s])
            return carry

        lax.fori_loop(0, local_src, source, 0, unroll=4)
        ship(0, c)
    build_operator(block_ref, multiples_ref, inner, local_src)
    near[...] = jnp.zeros_like(near)
    for s in range(local_src):
        spans[s] = radius_ref[s : s + 1, :]
    for c in range(chunks):
        own(0, c)
    for c in range(chunks):
        trace_side(0, c)
    for c in range(chunks):
        own(1, c)
    for c in range(chunks):
        trace_side(1, c)
    for phase in range(4):
        for c in range(chunks):
            await_all(phase, c, back_slabs if phase % 2 else out_slabs, send_sem)
    for place in range(2 * chunks):
        for side in range(2):

            @pl.when(sends[side])
            def _():
                rim(place, side).wait_send()


def finish_kernel(
    once_ref, last_ref, residual_ref, synthesis_ref, field_hbm, residual_hbm, done, ready_sem, done_sem, residual_sem
):
    local_src, receivers, _ = once_ref.shape
    width = last_ref.shape[2]
    start = receivers - width
    ready = pltpu.make_async_copy(once_ref.at[:, pl.ds(0, start), :], field_hbm.at[:, pl.ds(0, start), :], ready_sem)
    residual = pltpu.make_async_copy(residual_ref, residual_hbm, residual_sem)
    if start:
        ready.start()
    residual.start()

    def source(s, carry):
        done[s] = soft(once_ref[s, pl.ds(start, width), :] + tn_dot(last_ref[s], synthesis_ref[...]))
        pltpu.make_async_copy(done.at[s], field_hbm.at[s, pl.ds(start, width), :], done_sem).start()
        return carry

    lax.fori_loop(0, local_src, source, 0, unroll=2)
    pltpu.make_async_copy(done, field_hbm.at[:, pl.ds(start, width), :], done_sem).wait()
    residual.wait()
    if start:
        ready.wait()


def on_device(devices, start_field, recorded, multiples, block_index, radius):
    local_src, receivers, samples = start_field.shape
    local_freq = recorded.shape[0]
    rows = 2 * local_freq * devices
    width = 128
    chunks = receivers // width
    table = dft_table(local_freq * devices, samples)
    analysis = jnp.concatenate(halves(table.T), axis=0)
    high, low = halves(step_size * table.T)
    synthesis = jnp.concatenate([high, high, low], axis=0)
    vmem = pl.BlockSpec(memory_space=pltpu.VMEM)
    hbm = pl.BlockSpec(memory_space=pltpu.HBM)
    slab = pltpu.VMEM((2 * chunks, devices, local_freq * 2 * local_src, width), BF16)
    rim = pltpu.VMEM((2 * chunks, 2, RADIUS, rows, width), BF16)
    flat = pltpu.VMEM((rows * local_src, width), F32)
    field_shape = jax.ShapeDtypeStruct(start_field.shape, F32)
    residual_shape = jax.ShapeDtypeStruct((local_freq, receivers * NB, 2 * BS), F32)
    once, last, residual = pl.pallas_call(
        functools.partial(sweeps_kernel, devices, chunks, width),
        out_shape=(field_shape, jax.ShapeDtypeStruct((local_src, 3 * rows, width), BF16), residual_shape),
        in_specs=[pl.BlockSpec(memory_space=pltpu.SMEM), hbm] + [vmem] * 5,
        out_specs=(vmem, vmem, vmem),
        scratch_shapes=[
            pltpu.VMEM((chunks, local_src, width, samples), BF16),
            flat,
            flat,
            pltpu.VMEM((local_src + 2 * RADIUS, rows, width), F32),
            pltpu.VMEM((local_src, 1, receivers), jnp.int32),
            pltpu.VMEM((width * NB, 2 * BS), F32),
            pltpu.VMEM((local_freq, devices * 2 * local_src, NB * 2 * BS), BF16),
            slab,
            slab,
            slab,
            slab,
            rim,
            rim,
            pltpu.SemaphoreType.DMA((chunks,)),
            pltpu.SemaphoreType.DMA((4 * chunks,)),
            pltpu.SemaphoreType.DMA((4 * chunks,)),
            pltpu.SemaphoreType.DMA((2 * chunks, 2)),
            pltpu.SemaphoreType.DMA((2 * chunks, 2)),
        ],
        compiler_params=pltpu.CompilerParams(
            collective_id=0, has_side_effects=True, vmem_limit_bytes=28 << 20
        ),
    )(
        block_index, start_field, recorded.reshape(local_freq, receivers * NB, 2 * BS), multiples, radius,
        analysis, synthesis,
    )
    field, residual = pl.pallas_call(
        finish_kernel,
        out_shape=(field_shape, residual_shape),
        in_specs=[vmem] * 4,
        out_specs=(hbm, hbm),
        scratch_shapes=[
            pltpu.VMEM((local_src, width, samples), F32),
            pltpu.SemaphoreType.DMA,
            pltpu.SemaphoreType.DMA,
            pltpu.SemaphoreType.DMA,
        ],
        compiler_params=pltpu.CompilerParams(vmem_limit_bytes=24 << 20),
    )(once, last, residual, synthesis)
    return field, residual.reshape(recorded.shape)


def solution(mesh):
    placed = (
        P(("grp", "freq"), None, None),
        P(("grp", "freq"), None, None, None),
        P(("grp", "freq"), None, None, None, None),
        P(),
        P(("grp", "freq"), None),
    )
    return jax.shard_map(
        functools.partial(on_device, mesh.shape["freq"]),
        mesh=mesh,
        in_specs=placed,
        out_specs=(P(("grp", "freq"), None, None), P(("grp", "freq"), None, None, None)),
        check_vma=False,
    )
```

```python
import functools
import math

import jax
import jax.numpy as jnp
import numpy as np
from jax import lax
from jax.experimental import pallas as pl
from jax.experimental.pallas import tpu as pltpu
from jax.sharding import PartitionSpec as P

NB = 4
BS = 64
BANDS = 3
RADIUS = 4

step_size = 0.5
shrinkage = 0.05

BF16 = jnp.bfloat16
F32 = jnp.float32


def dft_table(freq_count, samples):
    phases = (np.arange(samples)[:, None] * (np.arange(freq_count) + 1)[None, :]) % samples
    angles = phases.astype(np.float64) * (2.0 * math.pi / samples)
    stacked = np.stack([np.cos(angles), -np.sin(angles)], axis=-1)
    return (stacked.reshape(samples, 2 * freq_count) / math.sqrt(samples)).astype(np.float32)


def halves(table):
    high = jnp.asarray(table).astype(BF16)
    low = (jnp.asarray(table) - high.astype(F32)).astype(BF16)
    return high, low


def soft(update):
    return update - jnp.clip(update, -shrinkage, shrinkage)


def nt_dot(a, b):
    return lax.dot_general(a, b, (((1,), (1,)), ((), ())), preferred_element_type=F32)


def tn_dot(a, b):
    return lax.dot_general(a, b, (((0,), (0,)), ((), ())), preferred_element_type=F32)


def build_operator(block_ref, multiples_ref, inner, local_src):
    parts = BS // local_src
    for f in range(multiples_ref.shape[0]):
        for j in range(NB):
            terms = [multiples_ref[f, j, b].astype(F32) for b in range(BANDS)]
            for m in range(NB):
                block = None
                for b in range(BANDS):
                    term = terms[b] * jnp.where(block_ref[j, b] == m, 1.0, 0.0)
                    block = term if block is None else block + term
                turned = jnp.concatenate([-block[:, BS:], block[:, :BS]], axis=1)
                for q in range(parts):
                    for c, half in enumerate((block, turned)):
                        row = ((m * parts + q) * 2 + c) * local_src
                        piece = half[q * local_src : (q + 1) * local_src]
                        inner[f, row : row + local_src, j * 2 * BS : (j + 1) * 2 * BS] = piece.astype(BF16)


def sweeps_kernel(
    devices, chunks, width,
    block_hbm, start_hbm, recorded_hbm, multiples_hbm, radius_hbm, analysis_hbm, synthesis_hbm,
    field_ref, last_ref, residual_ref,
    field, wide, flat, near, spans, given, inner, out_slabs, in_slabs, back_slabs, edge_slabs, rim_out, rim_in,
    block_ref, recorded_ref, multiples_ref, radius_ref, analysis_ref, synthesis_ref,
    load_sem, send_sem, recv_sem, rim_send, rim_recv, table_sem,
):
    me = lax.axis_index("freq")
    local_src = start_hbm.shape[0]
    local_freq = multiples_hbm.shape[0]
    rows = analysis_ref.shape[0] // 2
    block_cols = 2 * BS

    def load(c):
        return pltpu.make_async_copy(start_hbm.at[:, pl.ds(c * width, width), :], field.at[c], load_sem.at[c])

    load(0).start()
    tables = [
        pltpu.make_async_copy(source, target, table_sem.at[n])
        for n, (source, target) in enumerate(
            (
                (analysis_hbm, analysis_ref),
                (block_hbm, block_ref),
                (multiples_hbm, multiples_ref),
                (radius_hbm, radius_ref),
                (recorded_hbm, recorded_ref),
                (synthesis_hbm, synthesis_ref),
            )
        )
    ]
    tables[0].start()
    for c in range(1, chunks):
        load(c).start()
    for table in tables[1:]:
        table.start()
    barrier = pltpu.get_barrier_semaphore()
    for shift in range(1, devices):
        pl.semaphore_signal(
            barrier, inc=1, device_id={"freq": lax.rem(me + shift, devices)}, device_id_type=pl.DeviceIdType.MESH
        )

    def exchange(phase, c, sources, targets):
        slot = phase * chunks + c
        place = (phase // 2) * chunks + c

        def send(step, carry):
            peer = lax.rem(me + step, devices)
            pltpu.make_async_remote_copy(
                src_ref=sources.at[place, peer],
                dst_ref=targets.at[place, me],
                send_sem=send_sem.at[slot],
                recv_sem=recv_sem.at[slot],
                device_id={"freq": peer},
                device_id_type=pl.DeviceIdType.MESH,
            ).start()
            return carry

        lax.fori_loop(1, devices, send, 0)
        targets[place, me] = sources[place, me]

    def await_all(phase, c, refs, sems):
        whole = refs.at[(phase // 2) * chunks + c, pl.ds(0, devices - 1)]
        pltpu.make_async_copy(whole, whole, sems.at[phase * chunks + c]).wait()

    def rim(place, side):
        return pltpu.make_async_remote_copy(
            src_ref=rim_out.at[place, side],
            dst_ref=rim_in.at[place, side],
            send_sem=rim_send.at[place, side],
            recv_sem=rim_recv.at[place, side],
            device_id={"freq": lax.rem(me + (1 if side == 0 else devices - 1), devices)},
            device_id_type=pl.DeviceIdType.MESH,
        )

    sends = (me < devices - 1, me > 0)
    gets = (me > 0, me < devices - 1)

    def analyse(s, samples):
        both = nt_dot(analysis_ref[...], samples)
        wide[pl.ds(s, rows, stride=local_src), :] = both[:rows] + both[rows:]

    def ship(sweep, c):
        slabs = wide[...].reshape(devices, local_freq * 2 * local_src, width)
        out_slabs[sweep * chunks + c] = slabs.astype(BF16)
        if sweep == 0 and c == 0:
            pl.semaphore_wait(barrier, devices - 1)
        exchange(2 * sweep, c, out_slabs, in_slabs)

    def own(sweep, c):
        await_all(2 * sweep, c, in_slabs, recv_sem)
        arrived = in_slabs[sweep * chunks + c].astype(F32)
        backs = []
        for f in range(local_freq):
            part = arrived[:, f * 2 * local_src : (f + 1) * 2 * local_src]
            owned = part.reshape(devices * 2 * local_src, width).T.astype(BF16)
            predicted = jnp.dot(owned, inner[f], preferred_element_type=F32)
            given[...] = recorded_ref[f, pl.ds(c * width * NB, width * NB), :].astype(F32)
            narrow = []
            for j in range(NB):
                left = given[pl.ds(j, width, stride=NB), :] - predicted[:, j * block_cols : (j + 1) * block_cols]
                if sweep == 1:
                    residual_ref[f, pl.ds(c * width * NB + j, width, stride=NB), :] = left
                narrow.append(left.astype(BF16))
            back = nt_dot(inner[f], jnp.concatenate(narrow, axis=1))
            backs.append(back.reshape(devices, 2 * local_src, width))
        back = backs[0] if local_freq == 1 else jnp.concatenate(backs, axis=1)
        back_slabs[sweep * chunks + c] = back.astype(BF16)
        exchange(2 * sweep + 1, c, back_slabs, edge_slabs)

    def trace_side(sweep, c):
        place = sweep * chunks + c
        await_all(2 * sweep + 1, c, edge_slabs, recv_sem)
        flat[...] = edge_slabs[place].astype(F32).reshape(rows * local_src, width)
        for s in range(local_src):
            near[RADIUS + s] = flat[pl.ds(s, rows, stride=local_src), :]
        rim_out[place, 0] = near[local_src : local_src + RADIUS].astype(BF16)
        rim_out[place, 1] = near[RADIUS : 2 * RADIUS].astype(BF16)
        for side in range(2):

            @pl.when(sends[side])
            def _():
                rim(place, side).start()

        span_lanes = pl.ds(c * width, width)

        def source(s, carry):
            span = spans[s, :, span_lanes]
            box = near[s + RADIUS]
            smoothed = box
            for offset in range(1, RADIUS + 1):
                box = box + (near[s + RADIUS + offset] + near[s + RADIUS - offset])
                smoothed = jnp.where(span >= offset, box, smoothed)
            smoothed = smoothed * (1.0 / (2.0 * span.astype(F32) + 1.0))
            high = smoothed.astype(BF16)
            low = (smoothed - high.astype(F32)).astype(BF16)
            stack = jnp.concatenate([high, low, high], axis=0)
            if sweep == 0:
                update = soft(field[c, s].astype(F32) + tn_dot(stack, synthesis_ref[...]))
                field_ref[s, span_lanes, :] = update
                analyse(s, update.astype(BF16))
            elif c < chunks - 1:
                field_ref[s, span_lanes, :] = soft(field_ref[s, span_lanes, :] + tn_dot(stack, synthesis_ref[...]))
            else:
                last_ref[s] = stack
            return carry

        low_end = min(RADIUS, local_src)
        high_end = max(local_src - RADIUS, low_end)
        lax.fori_loop(low_end, high_end, source, 0, unroll=4)
        for side in range(2):

            @pl.when(gets[side])
            def _():
                rim(place, side).wait_recv()
                at = 0 if side == 0 else RADIUS + local_src
                near[at : at + RADIUS] = rim_in[place, side].astype(F32)

        lax.fori_loop(0, low_end, source, 0, unroll=4)
        lax.fori_loop(high_end, local_src, source, 0, unroll=4)
        if sweep == 0:
            ship(1, c)

    tables[0].wait()
    for c in range(chunks):
        load(c).wait()

        def source(s, carry):
            analyse(s, field[c, s])
            return carry

        lax.fori_loop(0, local_src, source, 0, unroll=4)
        ship(0, c)
    for table in tables[1:]:
        table.wait()
    build_operator(block_ref, multiples_ref, inner, local_src)
    near[...] = jnp.zeros_like(near)
    for s in range(local_src):
        spans[s] = radius_ref[s : s + 1, :]
    for c in range(chunks):
        own(0, c)
    for c in range(chunks):
        trace_side(0, c)
        if c:
            own(1, c - 1)
    own(1, chunks - 1)
    for c in range(chunks):
        trace_side(1, c)
    for phase in range(4):
        for c in range(chunks):
            await_all(phase, c, back_slabs if phase % 2 else out_slabs, send_sem)
    for place in range(2 * chunks):
        for side in range(2):

            @pl.when(sends[side])
            def _():
                rim(place, side).wait_send()


def finish_kernel(
    once_ref, last_ref, residual_ref, synthesis_hbm, field_hbm, residual_hbm,
    done, synthesis_ref, ready_sem, done_sem, residual_sem, table_sem,
):
    local_src, receivers, _ = once_ref.shape
    width = last_ref.shape[2]
    start = receivers - width
    ready = pltpu.make_async_copy(once_ref.at[:, pl.ds(0, start), :], field_hbm.at[:, pl.ds(0, start), :], ready_sem)
    residual = pltpu.make_async_copy(residual_ref, residual_hbm, residual_sem)
    table = pltpu.make_async_copy(synthesis_hbm, synthesis_ref, table_sem)
    table.start()
    if start:
        ready.start()
    residual.start()
    table.wait()

    def source(s, carry):
        done[s] = soft(once_ref[s, pl.ds(start, width), :] + tn_dot(last_ref[s], synthesis_ref[...]))
        pltpu.make_async_copy(done.at[s], field_hbm.at[s, pl.ds(start, width), :], done_sem).start()
        return carry

    lax.fori_loop(0, local_src, source, 0, unroll=4)
    pltpu.make_async_copy(done, field_hbm.at[:, pl.ds(start, width), :], done_sem).wait()
    residual.wait()
    if start:
        ready.wait()


def on_device(devices, start_field, recorded, multiples, block_index, radius):
    local_src, receivers, samples = start_field.shape
    local_freq = recorded.shape[0]
    rows = 2 * local_freq * devices
    width = 128
    chunks = receivers // width
    table = dft_table(local_freq * devices, samples)
    analysis = jnp.concatenate(halves(table.T), axis=0)
    high, low = halves(step_size * table.T)
    synthesis = jnp.concatenate([high, high, low], axis=0)
    vmem = pl.BlockSpec(memory_space=pltpu.VMEM)
    hbm = pl.BlockSpec(memory_space=pltpu.HBM)
    slab = pltpu.VMEM((2 * chunks, devices, local_freq * 2 * local_src, width), BF16)
    rim = pltpu.VMEM((2 * chunks, 2, RADIUS, rows, width), BF16)
    flat = pltpu.VMEM((rows * local_src, width), F32)
    field_shape = jax.ShapeDtypeStruct(start_field.shape, F32)
    residual_shape = jax.ShapeDtypeStruct((local_freq, receivers * NB, 2 * BS), F32)
    once, last, residual = pl.pallas_call(
        functools.partial(sweeps_kernel, devices, chunks, width),
        out_shape=(field_shape, jax.ShapeDtypeStruct((local_src, 3 * rows, width), BF16), residual_shape),
        in_specs=[hbm] * 7,
        out_specs=(vmem, vmem, vmem),
        scratch_shapes=[
            pltpu.VMEM((chunks, local_src, width, samples), BF16),
            flat,
            flat,
            pltpu.VMEM((local_src + 2 * RADIUS, rows, width), F32),
            pltpu.VMEM((local_src, 1, receivers), jnp.int32),
            pltpu.VMEM((width * NB, 2 * BS), F32),
            pltpu.VMEM((local_freq, devices * 2 * local_src, NB * 2 * BS), BF16),
            slab,
            slab,
            slab,
            slab,
            rim,
            rim,
            pltpu.SMEM(block_index.shape, block_index.dtype),
            pltpu.VMEM((local_freq, receivers * NB, 2 * BS), BF16),
            pltpu.VMEM(multiples.shape, BF16),
            pltpu.VMEM(radius.shape, radius.dtype),
            pltpu.VMEM(analysis.shape, BF16),
            pltpu.VMEM(synthesis.shape, BF16),
            pltpu.SemaphoreType.DMA((chunks,)),
            pltpu.SemaphoreType.DMA((4 * chunks,)),
            pltpu.SemaphoreType.DMA((4 * chunks,)),
            pltpu.SemaphoreType.DMA((2 * chunks, 2)),
            pltpu.SemaphoreType.DMA((2 * chunks, 2)),
            pltpu.SemaphoreType.DMA((6,)),
        ],
        compiler_params=pltpu.CompilerParams(
            collective_id=0, has_side_effects=True, vmem_limit_bytes=28 << 20
        ),
    )(
        *(
            pltpu.with_memory_space_constraint(value, pltpu.HBM)
            for value in (
                block_index, start_field, recorded.reshape(local_freq, receivers * NB, 2 * BS), multiples, radius,
                analysis, synthesis,
            )
        )
    )
    field, residual = pl.pallas_call(
        finish_kernel,
        out_shape=(field_shape, residual_shape),
        in_specs=[vmem] * 3 + [hbm],
        out_specs=(hbm, hbm),
        scratch_shapes=[
            pltpu.VMEM((local_src, width, samples), F32),
            pltpu.VMEM(synthesis.shape, BF16),
            pltpu.SemaphoreType.DMA,
            pltpu.SemaphoreType.DMA,
            pltpu.SemaphoreType.DMA,
            pltpu.SemaphoreType.DMA,
        ],
        compiler_params=pltpu.CompilerParams(vmem_limit_bytes=12 << 20),
    )(once, last, residual, pltpu.with_memory_space_constraint(synthesis, pltpu.HBM))
    return field, residual.reshape(recorded.shape)


def solution(mesh):
    placed = (
        P(("grp", "freq"), None, None),
        P(("grp", "freq"), None, None, None),
        P(("grp", "freq"), None, None, None, None),
        P(),
        P(("grp", "freq"), None),
    )
    return jax.shard_map(
        functools.partial(on_device, mesh.shape["freq"]),
        mesh=mesh,
        in_specs=placed,
        out_specs=(P(("grp", "freq"), None, None), P(("grp", "freq"), None, None, None)),
        check_vma=False,
    )
```

```python
import functools
import math

import jax
import jax.numpy as jnp
import numpy as np
from jax import lax
from jax.experimental import pallas as pl
from jax.experimental.pallas import tpu as pltpu
from jax.sharding import PartitionSpec as P

NB = 4
BS = 64
BANDS = 3
RADIUS = 4

step_size = 0.5
shrinkage = 0.05

BF16 = jnp.bfloat16
F32 = jnp.float32


def dft_table(freq_count, samples):
    phases = (np.arange(samples)[:, None] * (np.arange(freq_count) + 1)[None, :]) % samples
    angles = phases.astype(np.float64) * (2.0 * math.pi / samples)
    stacked = np.stack([np.cos(angles), -np.sin(angles)], axis=-1)
    return (stacked.reshape(samples, 2 * freq_count) / math.sqrt(samples)).astype(np.float32)


def halves(table):
    high = jnp.asarray(table).astype(BF16)
    low = (jnp.asarray(table) - high.astype(F32)).astype(BF16)
    return high, low


def soft(update):
    return update - jnp.clip(update, -shrinkage, shrinkage)


def nt_dot(a, b):
    return lax.dot_general(a, b, (((1,), (1,)), ((), ())), preferred_element_type=F32)


def tn_dot(a, b):
    return lax.dot_general(a, b, (((0,), (0,)), ((), ())), preferred_element_type=F32)


def build_operator(block_ref, multiples_ref, inner, local_src):
    parts = BS // local_src
    for f in range(multiples_ref.shape[0]):
        for j in range(NB):
            terms = [multiples_ref[f, j, b].astype(F32) for b in range(BANDS)]
            for m in range(NB):
                block = None
                for b in range(BANDS):
                    term = terms[b] * jnp.where(block_ref[j, b] == m, 1.0, 0.0)
                    block = term if block is None else block + term
                turned = jnp.concatenate([-block[:, BS:], block[:, :BS]], axis=1)
                for q in range(parts):
                    for c, half in enumerate((block, turned)):
                        row = ((m * parts + q) * 2 + c) * local_src
                        piece = half[q * local_src : (q + 1) * local_src]
                        inner[f, row : row + local_src, j * 2 * BS : (j + 1) * 2 * BS] = piece.astype(BF16)


def sweeps_kernel(
    devices, chunks, width,
    block_hbm, start_hbm, recorded_hbm, multiples_hbm, radius_hbm, analysis_hbm, synthesis_hbm,
    field_ref, last_ref, residual_ref,
    field, wide, flat, near, spans, given, inner, out_slabs, in_slabs, back_slabs, edge_slabs, rim_out, rim_in,
    block_ref, recorded_ref, multiples_ref, radius_ref, analysis_ref, synthesis_ref,
    load_sem, send_sem, recv_sem, rim_send, rim_recv, table_sem,
):
    me = lax.axis_index("freq")
    local_src = start_hbm.shape[0]
    local_freq = multiples_hbm.shape[0]
    rows = analysis_ref.shape[0] // 2
    block_cols = 2 * BS

    def load(c):
        return pltpu.make_async_copy(start_hbm.at[:, pl.ds(c * width, width), :], field.at[c], load_sem.at[c])

    load(0).start()
    tables = [
        pltpu.make_async_copy(source, target, table_sem.at[n])
        for n, (source, target) in enumerate(
            (
                (analysis_hbm, analysis_ref),
                (block_hbm, block_ref),
                (multiples_hbm, multiples_ref),
                (radius_hbm, radius_ref),
                (recorded_hbm, recorded_ref),
                (synthesis_hbm, synthesis_ref),
            )
        )
    ]
    tables[0].start()
    for c in range(1, chunks):
        load(c).start()
    for table in tables[1:]:
        table.start()
    barrier = pltpu.get_barrier_semaphore()
    for shift in range(1, devices):
        pl.semaphore_signal(
            barrier, inc=1, device_id={"freq": lax.rem(me + shift, devices)}, device_id_type=pl.DeviceIdType.MESH
        )

    def exchange(phase, c, sources, targets):
        slot = phase * chunks + c
        place = (phase // 2) * chunks + c

        def send(step, carry):
            peer = lax.rem(me + step, devices)
            pltpu.make_async_remote_copy(
                src_ref=sources.at[place, peer],
                dst_ref=targets.at[place, me],
                send_sem=send_sem.at[slot],
                recv_sem=recv_sem.at[slot],
                device_id={"freq": peer},
                device_id_type=pl.DeviceIdType.MESH,
            ).start()
            return carry

        lax.fori_loop(1, devices, send, 0)
        targets[place, me] = sources[place, me]

    def await_all(phase, c, refs, sems):
        whole = refs.at[(phase // 2) * chunks + c, pl.ds(0, devices - 1)]
        pltpu.make_async_copy(whole, whole, sems.at[phase * chunks + c]).wait()

    def rim(place, side):
        return pltpu.make_async_remote_copy(
            src_ref=rim_out.at[place, side],
            dst_ref=rim_in.at[place, side],
            send_sem=rim_send.at[place, side],
            recv_sem=rim_recv.at[place, side],
            device_id={"freq": lax.rem(me + (1 if side == 0 else devices - 1), devices)},
            device_id_type=pl.DeviceIdType.MESH,
        )

    sends = (me < devices - 1, me > 0)
    gets = (me > 0, me < devices - 1)

    def analyse(s, samples):
        both = nt_dot(analysis_ref[...], samples)
        wide[pl.ds(s, rows, stride=local_src), :] = both[:rows] + both[rows:]

    def ship(sweep, c):
        slabs = wide[...].reshape(devices, local_freq * 2 * local_src, width)
        out_slabs[sweep * chunks + c] = slabs.astype(BF16)
        if sweep == 0 and c == 0:
            pl.semaphore_wait(barrier, devices - 1)
        exchange(2 * sweep, c, out_slabs, in_slabs)

    def own(sweep, c):
        await_all(2 * sweep, c, in_slabs, recv_sem)
        arrived = in_slabs[sweep * chunks + c].astype(F32)
        backs = []
        for f in range(local_freq):
            part = arrived[:, f * 2 * local_src : (f + 1) * 2 * local_src]
            owned = part.reshape(devices * 2 * local_src, width).T.astype(BF16)
            predicted = jnp.dot(owned, inner[f], preferred_element_type=F32)
            given[...] = recorded_ref[f, pl.ds(c * width * NB, width * NB), :].astype(F32)
            narrow = []
            for j in range(NB):
                left = given[pl.ds(j, width, stride=NB), :] - predicted[:, j * block_cols : (j + 1) * block_cols]
                if sweep == 1:
                    residual_ref[f, pl.ds(c * width * NB + j, width, stride=NB), :] = left
                narrow.append(left.astype(BF16))
            back = nt_dot(inner[f], jnp.concatenate(narrow, axis=1))
            backs.append(back.reshape(devices, 2 * local_src, width))
        back = backs[0] if local_freq == 1 else jnp.concatenate(backs, axis=1)
        back_slabs[sweep * chunks + c] = back.astype(BF16)
        exchange(2 * sweep + 1, c, back_slabs, edge_slabs)

    def trace_side(sweep, c):
        place = sweep * chunks + c
        await_all(2 * sweep + 1, c, edge_slabs, recv_sem)
        flat[...] = edge_slabs[place].astype(F32).reshape(rows * local_src, width)
        for s in range(local_src):
            near[RADIUS + s] = flat[pl.ds(s, rows, stride=local_src), :]
        rim_out[place, 0] = near[local_src : local_src + RADIUS].astype(BF16)
        rim_out[place, 1] = near[RADIUS : 2 * RADIUS].astype(BF16)
        for side in range(2):

            @pl.when(sends[side])
            def _():
                rim(place, side).start()

        span_lanes = pl.ds(c * width, width)

        def source(s, carry):
            span = spans[s, :, span_lanes]
            box = near[s + RADIUS]
            smoothed = box
            for offset in range(1, RADIUS + 1):
                box = box + (near[s + RADIUS + offset] + near[s + RADIUS - offset])
                smoothed = jnp.where(span >= offset, box, smoothed)
            smoothed = smoothed * (1.0 / (2.0 * span.astype(F32) + 1.0))
            high = smoothed.astype(BF16)
            low = (smoothed - high.astype(F32)).astype(BF16)
            stack = jnp.concatenate([high, low, high], axis=0)
            if sweep == 0:
                update = soft(field[c, s].astype(F32) + tn_dot(stack, synthesis_ref[...]))
                field_ref[s, span_lanes, :] = update
                analyse(s, update.astype(BF16))
            elif c < chunks - 1:
                field_ref[s, span_lanes, :] = soft(field_ref[s, span_lanes, :] + tn_dot(stack, synthesis_ref[...]))
            else:
                last_ref[s] = stack
            return carry

        low_end = min(RADIUS, local_src)
        high_end = max(local_src - RADIUS, low_end)
        lax.fori_loop(low_end, high_end, source, 0, unroll=8)
        for side in range(2):

            @pl.when(gets[side])
            def _():
                rim(place, side).wait_recv()
                at = 0 if side == 0 else RADIUS + local_src
                near[at : at + RADIUS] = rim_in[place, side].astype(F32)

        lax.fori_loop(0, low_end, source, 0, unroll=4)
        lax.fori_loop(high_end, local_src, source, 0, unroll=4)
        if sweep == 0:
            ship(1, c)

    tables[0].wait()
    for c in range(chunks):
        load(c).wait()

        def source(s, carry):
            analyse(s, field[c, s])
            return carry

        lax.fori_loop(0, local_src, source, 0, unroll=8)
        ship(0, c)
    for table in tables[1:]:
        table.wait()
    build_operator(block_ref, multiples_ref, inner, local_src)
    near[...] = jnp.zeros_like(near)
    for s in range(local_src):
        spans[s] = radius_ref[s : s + 1, :]
    for c in range(chunks):
        own(0, c)
    for c in range(chunks):
        trace_side(0, c)
        if c:
            own(1, c - 1)
    own(1, chunks - 1)
    for c in range(chunks):
        trace_side(1, c)
    for phase in range(4):
        for c in range(chunks):
            await_all(phase, c, back_slabs if phase % 2 else out_slabs, send_sem)
    for place in range(2 * chunks):
        for side in range(2):

            @pl.when(sends[side])
            def _():
                rim(place, side).wait_send()


def finish_kernel(
    once_ref, last_ref, residual_ref, synthesis_hbm, field_hbm, residual_hbm,
    done, synthesis_ref, ready_sem, done_sem, residual_sem, table_sem,
):
    local_src, receivers, _ = once_ref.shape
    width = last_ref.shape[2]
    start = receivers - width
    ready = pltpu.make_async_copy(once_ref.at[:, pl.ds(0, start), :], field_hbm.at[:, pl.ds(0, start), :], ready_sem)
    residual = pltpu.make_async_copy(residual_ref, residual_hbm, residual_sem)
    table = pltpu.make_async_copy(synthesis_hbm, synthesis_ref, table_sem)
    table.start()
    if start:
        ready.start()
    residual.start()
    table.wait()

    def source(s, carry):
        done[s] = soft(once_ref[s, pl.ds(start, width), :] + tn_dot(last_ref[s], synthesis_ref[...]))
        pltpu.make_async_copy(done.at[s], field_hbm.at[s, pl.ds(start, width), :], done_sem).start()
        return carry

    lax.fori_loop(0, local_src, source, 0, unroll=8)
    pltpu.make_async_copy(done, field_hbm.at[:, pl.ds(start, width), :], done_sem).wait()
    residual.wait()
    if start:
        ready.wait()


def on_device(devices, start_field, recorded, multiples, block_index, radius):
    local_src, receivers, samples = start_field.shape
    local_freq = recorded.shape[0]
    rows = 2 * local_freq * devices
    width = 128
    chunks = receivers // width
    table = dft_table(local_freq * devices, samples)
    analysis = jnp.concatenate(halves(table.T), axis=0)
    high, low = halves(step_size * table.T)
    synthesis = jnp.concatenate([high, high, low], axis=0)
    vmem = pl.BlockSpec(memory_space=pltpu.VMEM)
    hbm = pl.BlockSpec(memory_space=pltpu.HBM)
    slab = pltpu.VMEM((2 * chunks, devices, local_freq * 2 * local_src, width), BF16)
    rim = pltpu.VMEM((2 * chunks, 2, RADIUS, rows, width), BF16)
    flat = pltpu.VMEM((rows * local_src, width), F32)
    field_shape = jax.ShapeDtypeStruct(start_field.shape, F32)
    residual_shape = jax.ShapeDtypeStruct((local_freq, receivers * NB, 2 * BS), F32)
    once, last, residual = pl.pallas_call(
        functools.partial(sweeps_kernel, devices, chunks, width),
        out_shape=(field_shape, jax.ShapeDtypeStruct((local_src, 3 * rows, width), BF16), residual_shape),
        in_specs=[hbm] * 7,
        out_specs=(vmem, vmem, vmem),
        scratch_shapes=[
            pltpu.VMEM((chunks, local_src, width, samples), BF16),
            flat,
            flat,
            pltpu.VMEM((local_src + 2 * RADIUS, rows, width), F32),
            pltpu.VMEM((local_src, 1, receivers), jnp.int32),
            pltpu.VMEM((width * NB, 2 * BS), F32),
            pltpu.VMEM((local_freq, devices * 2 * local_src, NB * 2 * BS), BF16),
            slab,
            slab,
            slab,
            slab,
            rim,
            rim,
            pltpu.SMEM(block_index.shape, block_index.dtype),
            pltpu.VMEM((local_freq, receivers * NB, 2 * BS), BF16),
            pltpu.VMEM(multiples.shape, BF16),
            pltpu.VMEM(radius.shape, radius.dtype),
            pltpu.VMEM(analysis.shape, BF16),
            pltpu.VMEM(synthesis.shape, BF16),
            pltpu.SemaphoreType.DMA((chunks,)),
            pltpu.SemaphoreType.DMA((4 * chunks,)),
            pltpu.SemaphoreType.DMA((4 * chunks,)),
            pltpu.SemaphoreType.DMA((2 * chunks, 2)),
            pltpu.SemaphoreType.DMA((2 * chunks, 2)),
            pltpu.SemaphoreType.DMA((6,)),
        ],
        compiler_params=pltpu.CompilerParams(
            collective_id=0, has_side_effects=True, vmem_limit_bytes=28 << 20
        ),
    )(
        *(
            pltpu.with_memory_space_constraint(value, pltpu.HBM)
            for value in (
                block_index, start_field, recorded.reshape(local_freq, receivers * NB, 2 * BS), multiples, radius,
                analysis, synthesis,
            )
        )
    )
    field, residual = pl.pallas_call(
        finish_kernel,
        out_shape=(field_shape, residual_shape),
        in_specs=[vmem] * 3 + [hbm],
        out_specs=(hbm, hbm),
        scratch_shapes=[
            pltpu.VMEM((local_src, width, samples), F32),
            pltpu.VMEM(synthesis.shape, BF16),
            pltpu.SemaphoreType.DMA,
            pltpu.SemaphoreType.DMA,
            pltpu.SemaphoreType.DMA,
            pltpu.SemaphoreType.DMA,
        ],
        compiler_params=pltpu.CompilerParams(vmem_limit_bytes=12 << 20),
    )(once, last, residual, pltpu.with_memory_space_constraint(synthesis, pltpu.HBM))
    return field, residual.reshape(recorded.shape)


def solution(mesh):
    placed = (
        P(("grp", "freq"), None, None),
        P(("grp", "freq"), None, None, None),
        P(("grp", "freq"), None, None, None, None),
        P(),
        P(("grp", "freq"), None),
    )
    return jax.shard_map(
        functools.partial(on_device, mesh.shape["freq"]),
        mesh=mesh,
        in_specs=placed,
        out_specs=(P(("grp", "freq"), None, None), P(("grp", "freq"), None, None, None)),
        check_vma=False,
    )
```
